32 devices in a mesh: groups: 2 (over x), tensor: 4 (over y, core), section: 4 (over z).
Axes of the slice: x: 2, y: 2, z: 4, core: 2. Of those that a mesh axis runs over, the one named last changes fastest.
Arguments:
- prompt: bfloat16 [128, 8192], P(('groups', 'section'), 'tensor'), parts along dimension 0, may hold values from -6 to 6
- norm_gain: float32 [8, 8192], P(('groups', 'section')), parts along dimension 0, may hold values from 0.5 to 1.5
- kept_ranks: int32 [8, 3], P(('groups', 'section')), parts along dimension 0, may hold values from 128 to 512, as said below
- gate_left: bfloat16 [8, 512, 8192], P('groups', 'tensor', 'section'), parts along dimension 0, may hold values from -0.0625 to 0.0625
- up_left: bfloat16 [8, 512, 8192], P('groups', 'tensor', 'section'), parts along dimension 0, may hold values from -0.0625 to 0.0625
- gate_right: bfloat16 [8, 512, 14336], P('groups', 'tensor', 'section'), parts along dimension 0, may hold values from -0.375 to 0.375
- up_right: bfloat16 [8, 512, 14336], P('groups', 'tensor', 'section'), parts along dimension 0, may hold values from -0.375 to 0.375
- down_left: bfloat16 [8, 512, 14336], P('groups', 'tensor', 'section'), parts along dimension 0, may hold values from -0.046875 to 0.046875
- down_right: bfloat16 [8, 8192, 512], P('groups', 'tensor', 'section'), parts along dimension 0, may hold values from -0.5 to 0.5
Outputs:
- final_stream: bfloat16 [128, 8192], P(('groups', 'section'), 'tensor'), parts along dimension 0
The draws below stay inside these ranges and needn't reach their ends.
There are 2 independent parts, one for each index of `groups`. The reference program is written for one: setup_inputs(seed, part) draws one part's arguments, and reference() takes and returns one part's arrays. A program takes and returns all parts, laid end to end along the dimension named above; each array names one. Nothing has to cross between parts.
Inputs may be any that keep to these rules, and one draw needn't show every extreme that they name: `kept_ranks`: column 0, 1, 2 holds the rank kept for the gate, up and down matrices; the value 512 occurs in every draw.
All inputs are finite; a program needn't handle non-finite values.
Results may differ from the reference program's by a relative error of at most 0.035.
Values may be sent and summed in bfloat16 or wider, within the bound.
No kernel may reach another device: no remote copies, remote signals or barrier semaphores. Data moves between devices by JAX's collectives and lax.ppermute only.
A program may use at most 128 MiB of HBM per device.

```python
import jax
import jax.numpy as jnp
from jax import lax

D = 8192
FF = 14336
RMAX = 512
LAYERS = 4
SPAN = 64


def draw_kept_ranks(key, part):
    key_draw, key_pick = jax.random.split(jax.random.fold_in(key, 7))
    drawn_ranks = jax.random.randint(key_draw, (LAYERS * 3,), RMAX // 4, RMAX + 1)
    chosen = jax.random.randint(key_pick, (), 0, LAYERS * 3)
    flat_ranks = jnp.where(jnp.arange(LAYERS * 3) == chosen, RMAX, drawn_ranks)
    return flat_ranks.reshape(LAYERS, 3).astype(jnp.int32)


def shard_levels(rng, extent, cuts, least, high):
    def one(position, shards_of):
        draws = jax.random.uniform(jax.random.fold_in(jax.random.fold_in(rng, 6), position), (shards_of,), jnp.float32, least / len(cuts), high / len(cuts))
        return jnp.repeat(jnp.exp(draws), extent[position] // shards_of).reshape((-1,) + (1,) * (len(extent) - position - 1))

    gain = one(*cuts[0])
    for cut in cuts[1:]:
        gain = gain * one(*cut)
    return gain


def bell_draw(key, dims, scale, bound, shards=(), kind=jnp.bfloat16):
    entries = jax.random.normal(key, dims, jnp.float32) * scale
    if len(shards) > 0:
        entries = shard_levels(key, dims, shards, -0.22, 0.18) * entries
    return jnp.clip(entries, min=-bound, max=bound).astype(kind)


def setup_inputs(seed: int = 0, part: int = 0) -> dict:
    keys = jax.random.split(jax.random.key(seed), 10)
    own_keys = jax.random.split(jax.random.fold_in(keys[9], part), 10)
    return {
        "prompt": bell_draw(own_keys[0], (SPAN, D), 1.0, 6.0, ((0, 4), (1, 4))),
        "norm_gain": jnp.clip(1.0 + 0.1 * jax.random.normal(own_keys[1], (LAYERS, D), jnp.float32), 0.5, 1.5),
        "kept_ranks": draw_kept_ranks(jax.random.fold_in(jax.random.fold_in(keys[9], part), 71), part),
        "gate_left": bell_draw(own_keys[3], (LAYERS, RMAX, D), D ** -0.5, 0.0625, ((1, 4), (2, 4))),
        "up_left": bell_draw(own_keys[4], (LAYERS, RMAX, D), D ** -0.5, 0.0625, ((1, 4), (2, 4))),
        "gate_right": bell_draw(own_keys[5], (LAYERS, RMAX, FF), (RMAX // 2) ** -0.5, 0.375, ((1, 4), (2, 4))),
        "up_right": bell_draw(own_keys[6], (LAYERS, RMAX, FF), (RMAX // 2) ** -0.5, 0.375, ((1, 4), (2, 4))),
        "down_left": bell_draw(own_keys[7], (LAYERS, RMAX, FF), FF ** -0.5, 0.046875, ((1, 4), (2, 4))),
        "down_right": bell_draw(own_keys[8], (LAYERS, D, RMAX), (RMAX // 4) ** -0.5, 0.5, ((1, 4), (2, 4))),
    }


def reference(prompt, norm_gain, kept_ranks, gate_left, up_left, gate_right, up_right, down_left, down_right):
    stream = prompt
    rank_axis = jnp.arange(RMAX, dtype=jnp.int32)
    for layer_index in range(LAYERS):
        float_stream = stream.astype(jnp.float32)
        variance = lax.optimization_barrier(jnp.mean(float_stream * float_stream, axis=-1, keepdims=True))
        normed = (float_stream * lax.rsqrt(variance + 1e-05) * norm_gain[layer_index]).astype(jnp.bfloat16)
        gate_mask = (rank_axis < kept_ranks[layer_index, 0]).astype(jnp.float32)
        up_mask = (rank_axis < kept_ranks[layer_index, 1]).astype(jnp.float32)
        down_mask = (rank_axis < kept_ranks[layer_index, 2]).astype(jnp.float32)
        gate_low = (jnp.dot(normed, gate_left[layer_index].T, preferred_element_type=jnp.float32) * gate_mask).astype(jnp.bfloat16)
        up_low = (jnp.dot(normed, up_left[layer_index].T, preferred_element_type=jnp.float32) * up_mask).astype(jnp.bfloat16)
        gate_values = jnp.dot(gate_low, gate_right[layer_index], preferred_element_type=jnp.float32)
        up_values = jnp.dot(up_low, up_right[layer_index], preferred_element_type=jnp.float32)
        hidden = (jax.nn.silu(gate_values) * up_values).astype(jnp.bfloat16)
        down_low = (jnp.dot(hidden, down_left[layer_index].T, preferred_element_type=jnp.float32) * down_mask).astype(jnp.bfloat16)
        branch = jnp.dot(down_low, down_right[layer_index].T, preferred_element_type=jnp.float32)
        stream = (float_stream + branch).astype(jnp.bfloat16)
    return stream
```

```python
import jax
import jax.numpy as jnp
from jax import lax
from jax.sharding import PartitionSpec as P

CORES = 2


def dot(left_side, right_side):
    return jnp.dot(left_side, right_side, preferred_element_type=jnp.float32)


def dot_last(left_side, right_side):
    return lax.dot_general(
        left_side, right_side, (((1,), (1,)), ((), ())), preferred_element_type=jnp.float32
    )


def swap_cores(block):
    ranks = range(lax.axis_size("tensor"))
    return lax.ppermute(block, "tensor", [(t, t ^ 1) for t in ranks])


def from_row(block, distance):
    tensor_count = lax.axis_size("tensor")
    shift = distance * CORES
    return lax.ppermute(
        block, "tensor", [(t, (t + shift) % tensor_count) for t in range(tensor_count)]
    )


def from_section(block, distance):
    count = lax.axis_size("section")
    return lax.ppermute(block, "section", [(s, (s + distance) % count) for s in range(count)])


def in_order(blocks, first, axis):
    count = len(blocks)
    if count == 1:
        return blocks[0]
    if count == 2:
        straight = jnp.concatenate(blocks, axis)
        turned = jnp.concatenate(blocks[::-1], axis)
        return jnp.where(first == 0, straight, turned)
    stacked = jnp.stack(blocks)
    places = (first - jnp.arange(count)) % count
    ordered = jnp.take(stacked, places, axis=0)
    return jnp.concatenate([ordered[i] for i in range(count)], axis)


def piece_of(block, index, count, axis):
    if count == 1:
        return block
    size = block.shape[axis] // count
    return lax.dynamic_slice_in_dim(block, index * size, size, axis)


def mirror(block, section_axis, tensor_axis):
    tensor_count, section_count = lax.axis_size("tensor"), lax.axis_size("section")
    ratio = tensor_count // section_count
    inner = lax.axis_index("tensor") % ratio
    arrived = []
    for shift in range(ratio):
        route = []
        for t in range(tensor_count):
            for s in range(section_count):
                target = ratio * s + (t % ratio + shift) % ratio
                route.append((t * section_count + s, target * section_count + t // ratio))
        piece = piece_of(block, (inner + shift) % ratio, ratio, section_axis)
        arrived.append(lax.ppermute(piece, ("tensor", "section"), route))
    return in_order(arrived, inner, tensor_axis)


def mirror_back(block, section_axis, tensor_axis):
    tensor_count, section_count = lax.axis_size("tensor"), lax.axis_size("section")
    ratio = tensor_count // section_count
    inner = lax.axis_index("tensor") % ratio
    arrived = []
    for shift in range(ratio):
        route = []
        for t in range(tensor_count):
            for s in range(section_count):
                target = ratio * s + (t % ratio + shift) % ratio
                route.append((t * section_count + s, target * section_count + t // ratio))
        piece = piece_of(block, (inner + shift) % ratio, ratio, tensor_axis)
        arrived.append(lax.ppermute(piece, ("tensor", "section"), route))
    return in_order(arrived, inner, section_axis)


def gather_rows(block, axis):
    rows = lax.axis_size("tensor") // CORES
    row = lax.axis_index("tensor") // CORES
    return in_order([block] + [from_row(block, k) for k in range(1, rows)], row, axis)


def gather_cores(block, axis):
    core = lax.axis_index("tensor") % CORES
    return in_order([block, swap_cores(block)], core, axis)


def sum_sections(block):
    total = block.astype(jnp.float32)
    arrived = [from_section(block, k) for k in range(1, lax.axis_size("section"))]
    for other in arrived:
        total = total + other.astype(jnp.float32)
    return total


def body(
    prompt, norm_gain, kept_ranks, gate_left, up_left, gate_right, up_right, down_left, down_right
):
    tensor_count, section_count = lax.axis_size("tensor"), lax.axis_size("section")
    tensor_rank, section_rank = lax.axis_index("tensor"), lax.axis_index("section")
    rows = tensor_count // CORES
    core, row = tensor_rank % CORES, tensor_rank // CORES
    layer_count = gate_left.shape[0]
    rank_block = gate_left.shape[1]
    width = norm_gain.shape[1]
    width_block = width // section_count
    ratio = tensor_count // section_count
    bf16, f32 = jnp.bfloat16, jnp.float32

    own = mirror(prompt, 0, 1)
    gain_piece = piece_of(norm_gain, tensor_rank, tensor_count, 1)
    settings = jnp.concatenate(
        [gain_piece, jnp.pad(kept_ranks.astype(f32), ((0, 0), (0, 125)))], 1
    )
    per_section = settings.shape[0]
    settings = mirror(jnp.tile(settings, (ratio, 1)), 0, 1)
    half = gather_rows(own, 0)
    settings = gather_rows(settings[None], 0)
    stream = gather_cores(half, 0)
    settings = gather_cores(settings[None], 0)
    first_right = mirror(down_right[:1], 2, 1)
    later_right = mirror(down_right[1:], 2, 1)

    column = jnp.arange(rank_block, dtype=jnp.int32) + tensor_rank * rank_block
    column = column.astype(f32)

    for layer in range(layer_count):
        owner = (layer // per_section) * ratio
        setting = settings[owner % CORES, owner // CORES, layer % per_section]
        parts = setting.reshape(ratio, -1)
        gain = parts[:, : width // tensor_count].reshape(-1)
        kept = parts[0, width // tensor_count :]

        float_stream = stream.astype(f32)
        squares = jnp.sum(float_stream * float_stream, -1, keepdims=True)
        high = squares.astype(bf16)
        low = (squares - high.astype(f32)).astype(bf16)
        weighted = (float_stream * gain).astype(bf16)
        gate_part = dot_last(weighted, gate_left[layer]).astype(bf16)
        up_part = dot_last(weighted, up_left[layer]).astype(bf16)
        tail = jnp.pad(jnp.concatenate([high, low], 1), ((0, 0), (0, 126)))
        total = sum_sections(jnp.concatenate([gate_part, up_part, tail], 1))
        squares = total[:, 2 * rank_block : 2 * rank_block + 1]
        squares = squares + total[:, 2 * rank_block + 1 : 2 * rank_block + 2]
        scale = lax.rsqrt(squares / width + 1e-05)
        gate_low = total[:, :rank_block] * scale * (column < kept[0]).astype(f32)
        up_low = total[:, rank_block : 2 * rank_block] * scale * (column < kept[1]).astype(f32)
        gate_low, up_low = gate_low.astype(bf16), up_low.astype(bf16)

        def products(side):
            gate = dot(gate_low, piece_of(gate_right[layer], side, CORES, 1))
            up = dot(up_low, piece_of(up_right[layer], side, CORES, 1))
            return jnp.stack([gate, up])

        sent = swap_cores(products(1 - core).astype(bf16))
        kept_sum = products(core) + sent.astype(f32)
        kept_low = kept_sum.astype(bf16)
        values = kept_low.astype(f32)
        for k in range(1, rows):
            values = values + from_row(kept_low, k).astype(f32)
        hidden = (jax.nn.silu(values[0]) * values[1]).astype(bf16)
        other = swap_cores(hidden)
        down = dot_last(hidden, piece_of(down_left[layer], core, CORES, 1))
        down = down + dot_last(other, piece_of(down_left[layer], 1 - core, CORES, 1))
        total = sum_sections(down.astype(bf16))
        down_low = (total * (column < kept[2]).astype(f32)).astype(bf16)

        right = first_right[0] if layer == 0 else later_right[layer - 1]
        kept_branch = dot_last(piece_of(down_low, core, CORES, 0), right)
        sent_branch = dot_last(piece_of(down_low, 1 - core, CORES, 0), right).astype(bf16)
        branch = (kept_branch + swap_cores(sent_branch).astype(f32)).astype(bf16)
        if layer < layer_count - 1:
            summed = half.astype(f32) + branch.astype(f32)
            for k in range(1, rows):
                summed = summed + from_row(branch, k).astype(f32)
            half = summed.astype(bf16)
            stream = gather_cores(half, 0)
        else:
            summed = piece_of(half, row, rows, 0).astype(f32)
            summed = summed + piece_of(branch, row, rows, 0).astype(f32)
            for k in range(1, rows):
                piece = piece_of(branch, (row + k) % rows, rows, 0)
                summed = summed + from_row(piece, k).astype(f32)
            return mirror_back(summed.astype(bf16), 0, 1)


def solution(mesh):
    in_specs = (
        P(("groups", "section"), "tensor"),
        P(("groups", "section"), None),
        P(("groups", "section"), None),
        P("groups", "tensor", "section"),
        P("groups", "tensor", "section"),
        P("groups", "tensor", "section"),
        P("groups", "tensor", "section"),
        P("groups", "tensor", "section"),
        P("groups", "tensor", "section"),
    )
    out_specs = P(("groups", "section"), "tensor")
    return jax.shard_map(body, mesh=mesh, in_specs=in_specs, out_specs=out_specs, check_vma=False)
```
